1024 devices in a mesh: dp: 16 (over x, y), expert: 64 (over z, core).
Axes of the slice: x: 4, y: 4, z: 32, core: 2. Of those that a mesh axis runs over, the one named last changes fastest.
Arguments:
- routing: int32 [131072, 2], P(('dp', 'expert')), may hold values from 0 to 63, all different within a row; in each aligned block of 128 rows (0 to 127, 128 to 255, ...) at most 6 rows name the same one
- gates: float32 [131072, 2], P(('dp', 'expert')), may hold values from 0.1 to 1
- hidden: bfloat16 [16, 64, 64, 6, 768], P('dp', 'expert'), may hold values from -6 to 6
- w_down: bfloat16 [64, 768, 2048], P('expert'), may hold values from -0.21875 to 0.21875
- dout: bfloat16 [131072, 2048], P(('dp', 'expert')), may hold values from -24 to 24
Outputs:
- combined: bfloat16 [131072, 2048], P(('dp', 'expert'))
- grad_gates: float32 [131072, 2], P(('dp', 'expert'))
- grad_hidden: bfloat16 [16, 64, 64, 6, 768], P('dp', 'expert')
- grad_down: float32 [64, 768, 2048], P('expert', None, 'dp')
The draws below stay inside these ranges and needn't reach their ends.
Inputs may be any that keep to these rules, and one draw needn't show every extreme that they name: `routing`: in each aligned block of 128 rows (the rows of one device) no expert is named by more than 6 picks, and in some block an expert is named by exactly 6.
All inputs are finite; a program needn't handle non-finite values.
Results may differ from the reference program's by a relative error of at most 0.013.
Values may be sent and summed in bfloat16 or wider, within the bound.
A program may use at most 64 MiB of HBM per device.

```python
import math
import jax
import jax.numpy as jnp
import numpy as np
from jax import lax

D = 2048
FF = 768
TOK_DEV = 128
TOP = 2
EXPERTS = 64
CAP = 6
TOKENS = 131072
N_DP = 16
N_EXPERT = 64


def raised(drawn, stream_key, source, target, shards_of, factor):
    def block_of(position):
        return (jnp.arange(drawn.shape[position]) // (drawn.shape[position] // shards_of)).reshape((-1,) + (1,) * (drawn.ndim - 1 - position))

    one_side = jax.random.permutation(stream_key, shards_of)[block_of(target)]
    other_side = (block_of(target) + shards_of // 2) % shards_of
    return jnp.where((block_of(source) == one_side) | (block_of(source) == other_side), factor * drawn, drawn)


def block_scale(key, dims, pieces, smallest, largest):
    def one(dim, blocks):
        draws = jax.random.uniform(jax.random.fold_in(jax.random.fold_in(key, 6), dim), (blocks,), jnp.float32, smallest / len(pieces), largest / len(pieces))
        return jnp.repeat(jnp.exp(draws), dims[dim] // blocks).reshape((-1,) + (1,) * (len(dims) - dim - 1))

    loudness = one(*pieces[0])
    for cut in pieces[1:]:
        loudness = loudness * one(*cut)
    return loudness


def routed_block(key, own, number, rows, number_of, top, reach, skew):
    sequence = jax.random.permutation(key, number_of)
    crowded, ordinary = shares(number_of, rows * top, reach, skew, True), shares(number_of, rows * top, reach, skew, False)
    places = jnp.arange(number_of)

    def named(lengths, offset_by):
        used = int((lengths > 0).sum())
        fixed = max(1, used // 4)
        shifted = fixed + (places - fixed + offset_by * (used - fixed)) % max(1, number_of - fixed)
        return jnp.zeros((number_of,), jnp.int32).at[sequence[jnp.where(places < fixed, places, shifted)]].set(jnp.asarray(lengths, jnp.int32))

    lengths = jnp.where(number % 4 == 0, named(crowded, number // 4), named(ordinary, number - number // 4 - 1))
    mixed = jax.random.permutation(jax.random.fold_in(own, 3), number_of)
    source_of, sink = mixed[0:number_of // 2 * 2:2], mixed[1:number_of // 2 * 2:2]
    slack = jnp.minimum(lengths[source_of] - 1, reach - lengths[sink]) // 2
    slack = jnp.where((source_of == sequence[0]) | (sink == sequence[0]) | (lengths[sink] == 0), 0, jnp.maximum(slack, 0))
    shifted = jax.random.randint(jax.random.fold_in(own, 4), (number_of // 2,), 0, 1 << 20) % (slack + 1)
    lengths = lengths.at[source_of].add(-shifted).at[sink].add(shifted)
    items = jnp.searchsorted(jnp.cumsum(lengths), jnp.arange(rows * top), side="right").astype(jnp.int32)
    grid = items.reshape(top, rows).T
    grid = grid[jax.random.permutation(jax.random.fold_in(own, 1), rows)]
    offset_by = jax.random.randint(jax.random.fold_in(own, 2), (rows, 1), 0, top)
    return jnp.take_along_axis(grid, (jnp.arange(top)[None, :] + offset_by) % top, axis=1)


def shares(count, total, reach, lean, full):
    loads = [(1 << 20) // math.isqrt(standing ** lean) + 1 for standing in range(1, count + 1)]
    largest = reach if full else min(reach, max(-(-total // count), total * loads[0] // sum(loads)))
    least = 1 if total - largest >= count - 1 else 0
    holding, surplus = [largest] + [least] * (count - 1), total - largest - least * (count - 1)
    while surplus > 0:
        candidates = [i for i in range(1, count) if holding[i] < largest] or [i for i in range(1, count) if holding[i] < reach]
        pool, left = sum([loads[i] for i in candidates]), surplus
        for i in candidates:
            more = min(reach - holding[i], max(1, left * loads[i] // pool), surplus)
            holding[i] = holding[i] + more
            surplus = surplus - more
    return np.array(holding)


def bell_draw(rng, shape, width, reach, cuts=(), kind=jnp.bfloat16):
    entries = width * jax.random.normal(rng, shape, jnp.float32)
    if cuts:
        entries = entries * block_scale(rng, shape, cuts, -0.22, 0.18)
    return jnp.clip(entries, -reach, reach).astype(kind)


def heavy_noise(key, dims, scale, bound, pieces, heavy, held_as=jnp.bfloat16):
    drawn = scale * jax.random.normal(key, dims, jnp.float32)
    if pieces:
        drawn = drawn * block_scale(key, dims, pieces, -0.22, 0.18)
    return jnp.clip(raised(drawn, jax.random.fold_in(key, 3), *heavy), -bound, bound).astype(held_as)


def setup_inputs(seed: int = 0) -> dict:
    streams_of = jax.random.split(jax.random.key(seed), 6)
    routing_keys = jax.random.split(jax.random.fold_in(streams_of[0], 1), TOKENS // TOK_DEV)
    routing_turns = jax.random.permutation(jax.random.fold_in(streams_of[0], 3), TOKENS // TOK_DEV)
    routing = jax.vmap(lambda own, number: routed_block(jax.random.fold_in(streams_of[0], 2), own, number, TOK_DEV, EXPERTS, TOP, CAP, 2))(routing_keys, routing_turns).reshape((TOKENS, TOP))
    gates = jnp.clip(jnp.exp(math.log(1.0) - 2.3025851 * jax.random.uniform(streams_of[1], (TOKENS, TOP), jnp.float32) ** block_scale(streams_of[1], (TOKENS, TOP), ((0, 1024),), -0.2, 0.2)), 0.1, 1.0)
    hidden = bell_draw(streams_of[2], (N_DP, EXPERTS, N_EXPERT, CAP, FF), 1.0, 6.0, ((0, 16), (1, 64)))
    w_down = bell_draw(streams_of[3], (EXPERTS, FF, D), FF ** -0.5, 0.21875, ((0, 64),))
    dout = heavy_noise(streams_of[4], (TOKENS, D), 1.0, 24.0, ((0, 1024),), (0, 1, 1024, 6.0))
    return dict(routing=routing, gates=gates, hidden=hidden, w_down=w_down, dout=dout)


def ranks_of(picks_block):
    onehot = (picks_block[:, None] == jnp.arange(EXPERTS, dtype=jnp.int32)[None, :]).astype(jnp.int32)
    before = jnp.cumsum(onehot, axis=0) - onehot
    return jnp.sum(before * onehot, axis=1).astype(jnp.int32)


def reference(routing, gates, hidden, w_down, dout):
    chosen_all = routing.reshape(N_DP, N_EXPERT, TOK_DEV * TOP)
    rankings = jax.vmap(jax.vmap(ranks_of))(chosen_all)
    gate_split = gates.reshape(N_DP, N_EXPERT, TOK_DEV, TOP)
    grad_split = dout.reshape(N_DP, N_EXPERT, TOK_DEV, D)
    weight_float = w_down.astype(jnp.float32)
    sources = jnp.arange(N_EXPERT, dtype=jnp.int32)[:, None]

    def per_group_step(total, item):
        hidden_block, chosen, ranking, gate_block, grad_block = item
        expert_out = jnp.einsum("esrf,efd->esrd", hidden_block.astype(jnp.float32), weight_float).astype(jnp.bfloat16)
        picked = expert_out[chosen, sources, ranking].reshape(N_EXPERT, TOK_DEV, TOP, D).astype(jnp.float32)
        mixture = jnp.sum(gate_block[..., None] * picked, axis=2).astype(jnp.bfloat16)
        grad_float = grad_block.astype(jnp.float32)
        gate_grads = jnp.sum(picked * grad_float[:, :, None, :], axis=3)
        scaled = (gate_block[..., None] * grad_float[:, :, None, :]).astype(jnp.bfloat16).reshape(N_EXPERT, TOK_DEV * TOP, D)
        slot_grads = jnp.zeros((EXPERTS, N_EXPERT, CAP, D), jnp.bfloat16).at[chosen, sources, ranking].set(scaled)
        hidden_grads = jnp.einsum("esrd,efd->esrf", slot_grads.astype(jnp.float32), weight_float).astype(jnp.bfloat16)
        partial_value = jnp.einsum("esrf,esrd->efd", hidden_block.astype(jnp.float32), slot_grads.astype(jnp.float32)).astype(jnp.bfloat16)
        return total + partial_value.astype(jnp.float32), (mixture, gate_grads, hidden_grads)

    start = jnp.zeros((EXPERTS, FF, D), jnp.float32)
    total, (mixture, gate_grads, hidden_grads) = lax.scan(per_group_step, start, (hidden, chosen_all, rankings, gate_split, grad_split))
    return mixture.reshape(TOKENS, D), gate_grads.reshape(TOKENS, TOP), hidden_grads, total
```

```python
import functools

import jax
import jax.numpy as jnp
from jax import lax
from jax.experimental import pallas as pl
from jax.experimental.pallas import tpu as pltpu
from jax.sharding import PartitionSpec as P

MESH = pl.DeviceIdType.MESH
F32 = jnp.float32
BF16 = jnp.bfloat16
PIECES = 8


def dot(a, b, contract):
    return lax.dot_general(a, b, ((contract[:1], contract[1:]), ((), ())), preferred_element_type=F32)


def perm(group, cap, shape_of, transposed):
    n = group * PIECES * cap
    row = lax.broadcasted_iota(jnp.int32, (n, n), 0)
    col = lax.broadcasted_iota(jnp.int32, (n, n), 1)
    if transposed:
        row, col = col, row
    line = row // group
    want = (row - line * group) * (PIECES * cap) + line
    return jnp.where(col == want, 1.0, 0.0).astype(BF16)


def to_blocks(matrix_t, rows_ref, blocks_ref, experts, cap, group):
    width = rows_ref.shape[1] // PIECES
    for g in range(experts // group):
        parts = []
        for j in range(PIECES):
            for r in range(cap):
                parts.append(rows_ref[r * experts + g * group:r * experts + (g + 1) * group, j * width:(j + 1) * width])
        stacked = jnp.concatenate(parts, axis=0)
        out = dot(matrix_t, stacked, (1, 0)).astype(BF16)
        blocks_ref[g * group:(g + 1) * group] = out.reshape(group, PIECES * cap, width)


def from_blocks(matrix, blocks_ref, rows_ref, experts, cap, group):
    width = rows_ref.shape[1] // PIECES
    for g in range(experts // group):
        stacked = blocks_ref[g * group:(g + 1) * group].reshape(group * PIECES * cap, width)
        out = dot(matrix, stacked, (1, 0)).astype(BF16)
        for j in range(PIECES):
            for r in range(cap):
                at = (j * cap + r) * group
                rows_ref[r * experts + g * group:r * experts + (g + 1) * group, j * width:(j + 1) * width] = out[at:at + group]


def column(row, n):
    a = lax.broadcasted_iota(jnp.int32, (n, n), 0)
    b = lax.broadcasted_iota(jnp.int32, (n, n), 1)
    return jnp.sum(jnp.where(a == b, row, jnp.zeros_like(row)), axis=1, keepdims=True)


def as_row(col, n):
    a = lax.broadcasted_iota(jnp.int32, (n, n), 0)
    b = lax.broadcasted_iota(jnp.int32, (n, n), 1)
    return jnp.sum(jnp.where(a == b, col, jnp.zeros_like(col)), axis=0, keepdims=True)


def before_kernel(experts, cap, group, routing_ref, gates_ref, dout_ref, blocks_ref, loc_ref, scaled, rows):
    top, tokens = routing_ref.shape
    number = lax.broadcasted_iota(jnp.int32, (experts, tokens), 0)
    hot = [number == routing_ref[k:k + 1, :] for k in range(top)]
    count = sum(jnp.where(h, 1.0, 0.0) for h in hot).astype(BF16)
    a = lax.broadcasted_iota(jnp.int32, (tokens, tokens), 0)
    b = lax.broadcasted_iota(jnp.int32, (tokens, tokens), 1)
    earlier = jnp.where(a < b, 1.0, 0.0).astype(BF16)
    before = dot(count, earlier, (1, 0))
    line = lax.broadcasted_iota(jnp.int32, (experts * cap, tokens), 0)
    onehot = []
    for k in range(top):
        rank = jnp.sum(jnp.where(hot[k], before, 0.0), axis=0, keepdims=True).astype(jnp.int32)
        loc = rank * experts + routing_ref[k:k + 1, :]
        loc_ref[k:k + 1, :] = loc
        onehot.append(jnp.where(line == loc, 1.0, 0.0).astype(BF16))
        scaled[k * tokens:(k + 1) * tokens, :] = (column(gates_ref[k:k + 1, :], tokens) * dout_ref[...].astype(F32)).astype(BF16)
    rows[...] = dot(jnp.concatenate(onehot, axis=1), scaled[...], (1, 0)).astype(BF16)
    to_blocks(perm(group, cap, None, True), rows, blocks_ref, experts, cap, group)


def after_kernel(experts, cap, group, blocks_ref, loc_ref, gates_ref, dout_ref, combined_ref, gg_ref, rows):
    top, tokens = loc_ref.shape
    from_blocks(perm(group, cap, None, False), blocks_ref, rows, experts, cap, group)
    place = lax.broadcasted_iota(jnp.int32, (tokens, experts * cap), 1)
    total = None
    grad = dout_ref[...].astype(F32)
    for k in range(top):
        onehot = jnp.where(place == column(loc_ref[k:k + 1, :], tokens), 1.0, 0.0).astype(BF16)
        picked = dot(onehot, rows[...], (1, 0))
        term = column(gates_ref[k:k + 1, :], tokens) * picked
        total = term if total is None else total + term
        gg_ref[k:k + 1, :] = as_row(jnp.sum(picked * grad, axis=1, keepdims=True), tokens)
    combined_ref[...] = total.astype(BF16)


def plan_of(half):
    groups = [[half]]
    top = half - 1
    while top >= 1:
        low = max(1, ((top - 1) // 4) * 4 + 1)
        groups.append(list(range(low, top + 1)))
        top = low - 1
    offset, total = {}, 0
    for d in range(1, half - 1):
        offset[d] = total
        total += half - 1 - d
    return groups, offset, max(total, 1)


def exchange_kernel(chips, groups_dp, cap, group, lead, at, a_ref, h_any, w_any, fb_ref, gh_ref, gd_ref,
                    a_in, h, w, sb, fa, rows, part, inbox, ring, ringh, rsem, ssem, fsem, psem, gsem, lsem):
    experts = 2 * chips
    half = chips // 2
    plan, offset, total = plan_of(half)
    me = lax.axis_index("expert")
    dp = lax.axis_index("dp")
    z = me // 2
    c = lax.rem(me, 2)
    other = 1 - c
    cols = fa.shape[2]
    hc = cols // 2

    loads = [pltpu.make_async_copy(s, d, lsem.at[i]) for i, (s, d) in enumerate(((a_ref, a_in), (h_any, h), (w_any, w)))]
    for load in loads:
        load.start()

    def chip(delta):
        return lax.rem(z + delta + chips, chips)

    barrier = pltpu.get_barrier_semaphore()
    near = [2 * chip(1) + c, 2 * chip(1) + other, 2 * chip(-1) + c, 2 * chip(-1) + other, 2 * z + other]
    for device in near:
        pl.semaphore_signal(barrier, inc=1, device_id={"expert": device}, device_id_type=MESH)
    for q in range(groups_dp - 1):
        pl.semaphore_signal(barrier, inc=1, device_id={"dp": lax.rem(dp + q + 1, groups_dp)}, device_id_type=MESH)
    loads[0].wait()
    pl.semaphore_wait(barrier, len(near) + groups_dp - 1)

    sources = (a_in, sb)
    finals = (fa, fb_ref)

    def remote(src, dst, send, recv, device):
        return pltpu.make_async_remote_copy(src_ref=src, dst_ref=dst, send_sem=send, recv_sem=recv, device_id=device, device_id_type=MESH)

    def sign(way):
        return 1 if way == 0 else -1

    def neighbour(way):
        return {"expert": 2 * chip(sign(way)) + c}

    def columns(way):
        return pl.ds(way * hc, hc)

    def final(s, way, d, src_of, is_half):
        origin = 2 * lax.rem(z - sign(way) * (d - 1) + chips, chips) + c
        dst = finals[s].at[origin, :, columns(way)] if is_half else finals[s].at[origin]
        for core in (c, other):
            remote(src_of(core), dst, ssem.at[s, way, 2], fsem.at[s], {"expert": 2 * chip(sign(way)) + core}).start()

    def hop_one(s):
        for g, ks in enumerate(plan):
            for k in reversed(ks):
                for way in (0, 1):
                    to = 2 * chip(sign(way) * k)
                    if k == half:
                        remote(sources[s].at[pl.ds(to, 2), :, columns(way)], ringh.at[s, way, pl.ds(0, 2)], ssem.at[s, way, 1],
                               rsem.at[s, way, 1, g], neighbour(way)).start()
                    elif k > 1:
                        i = offset[1] + k - 2
                        remote(sources[s].at[pl.ds(to, 2)], ring.at[s, way, pl.ds(2 * i, 2)], ssem.at[s, way, 0],
                               rsem.at[s, way, 1, g], neighbour(way)).start()
                    else:
                        final(s, way, 1, lambda core: sources[s].at[to + core], False)
        remote(sources[s].at[2 * z + other], finals[s].at[me], ssem.at[s, 0, 2], fsem.at[s], {"expert": 2 * z + other}).start()

    def hop(s, d):
        for g, ks in enumerate(plan):
            if ks[-1] < d:
                continue
            for way in (0, 1):
                if ks[-1] == half:
                    held = ringh.at[s, way, pl.ds(2 * (d - 2), 2)]
                    remote(held, held, ssem.at[s, way, 1], rsem.at[s, way, d - 1, g], neighbour(way)).wait_recv()
                    if d < half:
                        remote(held, ringh.at[s, way, pl.ds(2 * (d - 1), 2)], ssem.at[s, way, 1], rsem.at[s, way, d, g], neighbour(way)).start()
                    else:
                        final(s, way, d, lambda core: ringh.at[s, way, 2 * (d - 2) + core], True)
                    continue
                low = max(ks[0], d)
                first = offset[d - 1] + low - d
                held = ring.at[s, way, pl.ds(2 * first, 2 * (ks[-1] - low + 1))]
                remote(held, held, ssem.at[s, way, 0], rsem.at[s, way, d - 1, g], neighbour(way)).wait_recv()
                onward = max(ks[0], d + 1)
                if onward <= ks[-1]:
                    size = 2 * (ks[-1] - onward + 1)
                    remote(ring.at[s, way, pl.ds(2 * (offset[d - 1] + onward - d), size)],
                           ring.at[s, way, pl.ds(2 * (offset[d] + onward - d - 1), size)],
                           ssem.at[s, way, 0], rsem.at[s, way, d, g], neighbour(way)).start()
                if low == d:
                    final(s, way, d, lambda core: ring.at[s, way, 2 * first + core], False)

    def arrived(s):
        remote(finals[s].at[pl.ds(0, experts - 1)], finals[s].at[pl.ds(0, experts - 1)], ssem.at[s, 0, 2], fsem.at[s], neighbour(0)).wait_recv()

    def forward():
        loads[1].wait()
        loads[2].wait()
        width = w.shape[1] // 4
        for i in range(4):
            rows[:, i * width:(i + 1) * width] = dot(h[...], w[:, i * width:(i + 1) * width], (1, 0)).astype(BF16)
        to_blocks(perm(group, cap, None, True), rows, sb, experts, cap, group)
        fb_ref[me] = sb[me]

    def unpack():
        arrived(0)
        fa[me] = a_in[me]
        from_blocks(perm(group, cap, None, False), fa, rows, experts, cap, group)

    def hidden_grads():
        gh_ref[...] = dot(rows[...], w[...], (1, 1)).astype(BF16)

    def weight_grads():
        piece = part.shape[2]
        for i in range(groups_dp // 2):
            both = dot(h[...], rows[:, 2 * i * piece:2 * (i + 1) * piece], (0, 0)).astype(BF16)
            part[2 * i] = both[:, :piece]
            part[2 * i + 1] = both[:, piece:]
        for q in range(groups_dp - 1):
            to = lax.rem(dp + q + 1, groups_dp)
            remote(part.at[to], inbox.at[q], psem, gsem, {"dp": to}).start()

    work = {at: unpack, at + 1: hidden_grads, at + 2: weight_grads}
    hop_one(0)
    forward()
    for d in range(2, lead + 1):
        hop(0, d)
    hop_one(1)
    for i in range(2, half + 1):
        if lead + i - 1 <= half:
            hop(0, lead + i - 1)
        hop(1, i)
        if i in work:
            work.pop(i)()
    for job in work.values():
        job()

    remote(inbox, inbox, psem, gsem, {"dp": dp}).wait_recv()
    total_grad = part[dp].astype(F32)
    for q in range(groups_dp - 1):
        total_grad = total_grad + inbox[q].astype(F32)
    gd_ref[...] = total_grad
    arrived(1)
    for s in (0, 1):
        for way in (0, 1):
            if half > 2:
                remote(ring.at[s, way], ring.at[s, way], ssem.at[s, way, 0], rsem.at[s, way, 1, 0], neighbour(way)).wait_send()
            remote(ringh.at[s, way], ringh.at[s, way], ssem.at[s, way, 1], rsem.at[s, way, 1, 0], neighbour(way)).wait_send()
            sent = finals[s].at[pl.ds(0, 2 * (half - 1) + 1 + (1 if way == 0 else 0))]
            remote(sent, sent, ssem.at[s, way, 2], fsem.at[s], neighbour(way)).wait_send()
    remote(inbox, inbox, psem, gsem, {"dp": dp}).wait_send()


def on_device(chips, groups_dp, lead, at, routing, gates, hidden, w_down, dout):
    experts = 2 * chips
    cap, units = hidden.shape[3], hidden.shape[4]
    width = w_down.shape[2]
    tokens, top = routing.shape
    group = min(16, experts)
    cols = width // PIECES
    block = (experts, PIECES * cap, cols)
    routing_t, gates_t = routing.T, gates.T
    h = jnp.transpose(hidden[0, 0], (1, 0, 2)).reshape(cap * experts, units)
    vmem = pl.BlockSpec(memory_space=pltpu.VMEM)
    anywhere = pl.BlockSpec(memory_space=pl.ANY)

    blocks, loc = pl.pallas_call(
        functools.partial(before_kernel, experts, cap, group),
        out_shape=(jax.ShapeDtypeStruct(block, BF16), jax.ShapeDtypeStruct((top, tokens), jnp.int32)),
        in_specs=[vmem] * 3,
        out_specs=(vmem, vmem),
        scratch_shapes=[pltpu.VMEM((top * tokens, width), BF16), pltpu.VMEM((experts * cap, width), BF16)],
        name="pack",
    )(routing_t, gates_t, dout)

    half = chips // 2
    plan, _, total = plan_of(half)
    piece = width // groups_dp
    back, grad_hidden, grad_down = pl.pallas_call(
        functools.partial(exchange_kernel, chips, groups_dp, cap, group, lead, at),
        out_shape=(jax.ShapeDtypeStruct(block, BF16), jax.ShapeDtypeStruct((cap * experts, units), BF16),
                   jax.ShapeDtypeStruct((units, piece), F32)),
        in_specs=[anywhere] * 3,
        out_specs=(vmem, vmem, vmem),
        scratch_shapes=[
            pltpu.VMEM(block, BF16),
            pltpu.VMEM((cap * experts, units), BF16),
            pltpu.VMEM((units, width), BF16),
            pltpu.VMEM(block, BF16),
            pltpu.VMEM(block, BF16),
            pltpu.VMEM((cap * experts, width), BF16),
            pltpu.VMEM((groups_dp, units, piece), BF16),
            pltpu.VMEM((groups_dp - 1, units, piece), BF16),
            pltpu.VMEM((2, 2, 2 * total, PIECES * cap, cols), BF16),
            pltpu.VMEM((2, 2, 2 * (half - 1), PIECES * cap, cols // 2), BF16),
            pltpu.SemaphoreType.DMA((2, 2, half, len(plan))),
            pltpu.SemaphoreType.DMA((2, 2, 3)),
            pltpu.SemaphoreType.DMA((2,)),
            pltpu.SemaphoreType.DMA,
            pltpu.SemaphoreType.DMA,
            pltpu.SemaphoreType.DMA((3,)),
        ],
        compiler_params=pltpu.CompilerParams(collective_id=0, has_side_effects=True, vmem_limit_bytes=62 * 1024 * 1024),
        name="exchange",
    )(blocks, h, w_down[0])

    combined, grad_gates = pl.pallas_call(
        functools.partial(after_kernel, experts, cap, group),
        out_shape=(jax.ShapeDtypeStruct((tokens, width), BF16), jax.ShapeDtypeStruct((top, tokens), F32)),
        in_specs=[vmem] * 4,
        out_specs=(vmem, vmem),
        scratch_shapes=[pltpu.VMEM((experts * cap, width), BF16)],
        name="combine",
    )(back, loc, gates_t, dout)
    grad_hidden = jnp.transpose(grad_hidden.reshape(cap, experts, units), (1, 0, 2))
    return combined, grad_gates.T, grad_hidden[None, None], grad_down[None]


def solution(mesh):
    chips, groups_dp = mesh.shape["expert"] // 2, mesh.shape["dp"]
    half = chips // 2
    lead = max(1, half - 4)
    at = half - lead + 4
    placed = (
        P(("dp", "expert"), None),
        P(("dp", "expert"), None),
        P("dp", "expert", None, None, None),
        P("expert", None, None),
        P(("dp", "expert"), None),
    )
    return jax.shard_map(
        functools.partial(on_device, chips, groups_dp, lead, at),
        mesh=mesh,
        in_specs=placed,
        out_specs=(
            P(("dp", "expert"), None),
            P(("dp", "expert"), None),
            P("dp", "expert", None, None, None),
            P("expert", None, "dp"),
        ),
        check_vma=False,
    )
```

```python
import functools

import jax
import jax.numpy as jnp
from jax import lax
from jax.experimental import pallas as pl
from jax.experimental.pallas import tpu as pltpu
from jax.sharding import PartitionSpec as P

MESH = pl.DeviceIdType.MESH
F32 = jnp.float32
BF16 = jnp.bfloat16
PIECES = 8


def dot(a, b, contract):
    return lax.dot_general(a, b, ((contract[:1], contract[1:]), ((), ())), preferred_element_type=F32)


def perm(group, cap, shape_of, transposed):
    n = group * PIECES * cap
    row = lax.broadcasted_iota(jnp.int32, (n, n), 0)
    col = lax.broadcasted_iota(jnp.int32, (n, n), 1)
    if transposed:
        row, col = col, row
    line = row // group
    want = (row - line * group) * (PIECES * cap) + line
    return jnp.where(col == want, 1.0, 0.0).astype(BF16)


def to_blocks(matrix_t, rows_ref, blocks_ref, experts, cap, group):
    width = rows_ref.shape[1] // PIECES
    for g in range(experts // group):
        parts = []
        for j in range(PIECES):
            for r in range(cap):
                parts.append(rows_ref[r * experts + g * group:r * experts + (g + 1) * group, j * width:(j + 1) * width])
        stacked = jnp.concatenate(parts, axis=0)
        out = dot(matrix_t, stacked, (1, 0)).astype(BF16)
        blocks_ref[g * group:(g + 1) * group] = out.reshape(group, PIECES * cap, width)


def from_blocks(matrix, blocks_ref, rows_ref, experts, cap, group):
    width = rows_ref.shape[1] // PIECES
    for g in range(experts // group):
        stacked = blocks_ref[g * group:(g + 1) * group].reshape(group * PIECES * cap, width)
        out = dot(matrix, stacked, (1, 0)).astype(BF16)
        for j in range(PIECES):
            for r in range(cap):
                at = (j * cap + r) * group
                rows_ref[r * experts + g * group:r * experts + (g + 1) * group, j * width:(j + 1) * width] = out[at:at + group]


def column(row, n):
    a = lax.broadcasted_iota(jnp.int32, (n, n), 0)
    b = lax.broadcasted_iota(jnp.int32, (n, n), 1)
    return jnp.sum(jnp.where(a == b, row, jnp.zeros_like(row)), axis=1, keepdims=True)


def as_row(col, n):
    a = lax.broadcasted_iota(jnp.int32, (n, n), 0)
    b = lax.broadcasted_iota(jnp.int32, (n, n), 1)
    return jnp.sum(jnp.where(a == b, col, jnp.zeros_like(col)), axis=0, keepdims=True)


def before_kernel(experts, cap, group, routing_ref, gates_ref, dout_ref, blocks_ref, loc_ref, scaled, rows):
    top, tokens = routing_ref.shape
    number = lax.broadcasted_iota(jnp.int32, (experts, tokens), 0)
    hot = [number == routing_ref[k:k + 1, :] for k in range(top)]
    count = sum(jnp.where(h, 1.0, 0.0) for h in hot).astype(BF16)
    a = lax.broadcasted_iota(jnp.int32, (tokens, tokens), 0)
    b = lax.broadcasted_iota(jnp.int32, (tokens, tokens), 1)
    earlier = jnp.where(a < b, 1.0, 0.0).astype(BF16)
    before = dot(count, earlier, (1, 0))
    line = lax.broadcasted_iota(jnp.int32, (experts * cap, tokens), 0)
    onehot = []
    for k in range(top):
        rank = jnp.sum(jnp.where(hot[k], before, 0.0), axis=0, keepdims=True).astype(jnp.int32)
        loc = rank * experts + routing_ref[k:k + 1, :]
        loc_ref[k:k + 1, :] = loc
        onehot.append(jnp.where(line == loc, 1.0, 0.0).astype(BF16))
        scaled[k * tokens:(k + 1) * tokens, :] = (column(gates_ref[k:k + 1, :], tokens) * dout_ref[...].astype(F32)).astype(BF16)
    rows[...] = dot(jnp.concatenate(onehot, axis=1), scaled[...], (1, 0)).astype(BF16)
    to_blocks(perm(group, cap, None, True), rows, blocks_ref, experts, cap, group)


def after_kernel(experts, cap, group, blocks_ref, loc_ref, gates_ref, dout_ref, combined_ref, gg_ref, rows):
    top, tokens = loc_ref.shape
    from_blocks(perm(group, cap, None, False), blocks_ref, rows, experts, cap, group)
    place = lax.broadcasted_iota(jnp.int32, (tokens, experts * cap), 1)
    total = None
    grad = dout_ref[...].astype(F32)
    for k in range(top):
        onehot = jnp.where(place == column(loc_ref[k:k + 1, :], tokens), 1.0, 0.0).astype(BF16)
        picked = dot(onehot, rows[...], (1, 0))
        term = column(gates_ref[k:k + 1, :], tokens) * picked
        total = term if total is None else total + term
        gg_ref[k:k + 1, :] = as_row(jnp.sum(picked * grad, axis=1, keepdims=True), tokens)
    combined_ref[...] = total.astype(BF16)


def plan_of(half):
    groups = [[half]]
    top = half - 1
    while top >= 1:
        low = max(1, ((top - 1) // 4) * 4 + 1)
        groups.append(list(range(low, top + 1)))
        top = low - 1
    offset, total = {}, 0
    for d in range(1, half - 1):
        offset[d] = total
        total += half - 1 - d
    return groups, offset, max(total, 1)


def exchange_kernel(chips, groups_dp, cap, group, lead, a_ref, h_any, w_any, fb_ref, gh_ref, gd_ref,
                    a_in, h, ht, w, sb, fa, rows, part, inbox, ring, ringh, rsem, ssem, fsem, psem, gsem, lsem):
    experts = 2 * chips
    half = chips // 2
    plan, offset, total = plan_of(half)
    me = lax.axis_index("expert")
    dp = lax.axis_index("dp")
    z = me // 2
    c = lax.rem(me, 2)
    other = 1 - c
    cols = fa.shape[2]
    hc = cols // 2

    loads = [pltpu.make_async_copy(s, d, lsem.at[i]) for i, (s, d) in enumerate(((a_ref, a_in), (h_any, h), (w_any, w)))]
    for load in loads:
        load.start()

    def chip(delta):
        return lax.rem(z + delta + chips, chips)

    barrier = pltpu.get_barrier_semaphore()
    near = [2 * chip(1) + c, 2 * chip(1) + other, 2 * chip(-1) + c, 2 * chip(-1) + other, 2 * z + other]
    for device in near:
        pl.semaphore_signal(barrier, inc=1, device_id={"expert": device}, device_id_type=MESH)
    for q in range(groups_dp - 1):
        pl.semaphore_signal(barrier, inc=1, device_id={"dp": lax.rem(dp + q + 1, groups_dp)}, device_id_type=MESH)
    loads[0].wait()
    pl.semaphore_wait(barrier, len(near) + groups_dp - 1)

    sources = (a_in, sb)
    finals = (fa, fb_ref)

    def remote(src, dst, send, recv, device):
        return pltpu.make_async_remote_copy(src_ref=src, dst_ref=dst, send_sem=send, recv_sem=recv, device_id=device, device_id_type=MESH)

    def sign(way):
        return 1 if way == 0 else -1

    def neighbour(way):
        return {"expert": 2 * chip(sign(way)) + c}

    def columns(way):
        return pl.ds(way * hc, hc)

    def final(s, way, d, src_of, is_half):
        origin = 2 * lax.rem(z - sign(way) * (d - 1) + chips, chips) + c
        dst = finals[s].at[origin, :, columns(way)] if is_half else finals[s].at[origin]
        for core in (c, other):
            remote(src_of(core), dst, ssem.at[s, way, 2], fsem.at[s], {"expert": 2 * chip(sign(way)) + core}).start()

    def begin(s, g):
        for k in reversed(plan[g]):
            for way in (0, 1):
                to = 2 * chip(sign(way) * k)
                if k == half:
                    remote(sources[s].at[pl.ds(to, 2), :, columns(way)], ringh.at[s, way, pl.ds(0, 2)], ssem.at[s, way, 1],
                           rsem.at[s, way, 1, g], neighbour(way)).start()
                elif k > 1:
                    i = offset[1] + k - 2
                    remote(sources[s].at[pl.ds(to, 2)], ring.at[s, way, pl.ds(2 * i, 2)], ssem.at[s, way, 0],
                           rsem.at[s, way, 1, g], neighbour(way)).start()
                else:
                    final(s, way, 1, lambda core: sources[s].at[to + core], False)
        if plan[g][0] == 1:
            remote(sources[s].at[2 * z + other], finals[s].at[me], ssem.at[s, 0, 2], fsem.at[s], {"expert": 2 * z + other}).start()

    def onward(s, g, d):
        ks = plan[g]
        for way in (0, 1):
            if ks[-1] == half:
                held = ringh.at[s, way, pl.ds(2 * (d - 2), 2)]
                remote(held, held, ssem.at[s, way, 1], rsem.at[s, way, d - 1, g], neighbour(way)).wait_recv()
                if d < half:
                    remote(held, ringh.at[s, way, pl.ds(2 * (d - 1), 2)], ssem.at[s, way, 1], rsem.at[s, way, d, g], neighbour(way)).start()
                else:
                    final(s, way, d, lambda core: ringh.at[s, way, 2 * (d - 2) + core], True)
                continue
            low = max(ks[0], d)
            first = offset[d - 1] + low - d
            held = ring.at[s, way, pl.ds(2 * first, 2 * (ks[-1] - low + 1))]
            remote(held, held, ssem.at[s, way, 0], rsem.at[s, way, d - 1, g], neighbour(way)).wait_recv()
            rest = max(ks[0], d + 1)
            if rest <= ks[-1]:
                size = 2 * (ks[-1] - rest + 1)
                remote(ring.at[s, way, pl.ds(2 * (offset[d - 1] + rest - d), size)],
                       ring.at[s, way, pl.ds(2 * (offset[d] + rest - d - 1), size)],
                       ssem.at[s, way, 0], rsem.at[s, way, d, g], neighbour(way)).start()
            if low == d:
                final(s, way, d, lambda core: ring.at[s, way, 2 * first + core], False)

    def arrived(s):
        remote(finals[s].at[pl.ds(0, experts - 1)], finals[s].at[pl.ds(0, experts - 1)], ssem.at[s, 0, 2], fsem.at[s], neighbour(0)).wait_recv()

    def forward():
        loads[1].wait()
        loads[2].wait()
        width = w.shape[1] // 4
        for i in range(4):
            rows[:, i * width:(i + 1) * width] = dot(h[...], w[:, i * width:(i + 1) * width], (1, 0)).astype(BF16)
        to_blocks(perm(group, cap, None, True), rows, sb, experts, cap, group)
        fb_ref[me] = sb[me]

    def flip():
        ht[...] = h[...].T

    def unpack():
        arrived(0)
        fa[me] = a_in[me]
        from_blocks(perm(group, cap, None, False), fa, rows, experts, cap, group)

    def hidden_grads():
        gh_ref[...] = dot(rows[...], w[...], (1, 1)).astype(BF16)

    def weight_grads(step):
        piece, size = part.shape[2], part.shape[1] // 2
        lines = pl.ds(step * size, size)
        for i in range(groups_dp // 2):
            both = dot(ht[lines, :], rows[:, 2 * i * piece:2 * (i + 1) * piece], (1, 0)).astype(BF16)
            part[2 * i, lines, :] = both[:, :piece]
            part[2 * i + 1, lines, :] = both[:, piece:]
        for q in range(groups_dp - 1):
            to = lax.rem(dp + q + 1, groups_dp)
            remote(part.at[to, lines, :], inbox.at[q, lines, :], psem, gsem, {"dp": to}).start()

    def grads():
        unpack()
        weight_grads(0)
        weight_grads(1)

    work = {(1, len(plan) - 1): forward, (3, len(plan) - 1): flip, (half + 1, min(1, len(plan) - 2)): grads, (half + 2, 1): hidden_grads}
    for i in range(1, lead + half + 1):
        for g, ks in enumerate(plan):
            for s in (0, 1):
                d = i - (0 if s == 0 else lead + half - ks[-1])
                if d == 1:
                    begin(s, g)
                elif 1 < d <= ks[-1]:
                    onward(s, g, d)
            if (i, g) in work:
                work.pop((i, g))()
    for job in work.values():
        job()

    remote(inbox, inbox, psem, gsem, {"dp": dp}).wait_recv()
    total_grad = part[dp].astype(F32)
    for q in range(groups_dp - 1):
        total_grad = total_grad + inbox[q].astype(F32)
    gd_ref[...] = total_grad
    arrived(1)
    for s in (0, 1):
        for way in (0, 1):
            if half > 2:
                remote(ring.at[s, way], ring.at[s, way], ssem.at[s, way, 0], rsem.at[s, way, 1, 0], neighbour(way)).wait_send()
            remote(ringh.at[s, way], ringh.at[s, way], ssem.at[s, way, 1], rsem.at[s, way, 1, 0], neighbour(way)).wait_send()
            sent = finals[s].at[pl.ds(0, 2 * (half - 1) + 1 + (1 if way == 0 else 0))]
            remote(sent, sent, ssem.at[s, way, 2], fsem.at[s], neighbour(way)).wait_send()
    remote(inbox, inbox, psem, gsem, {"dp": dp}).wait_send()


def on_device(chips, groups_dp, lead, routing, gates, hidden, w_down, dout):
    experts = 2 * chips
    cap, units = hidden.shape[3], hidden.shape[4]
    width = w_down.shape[2]
    tokens, top = routing.shape
    group = min(16, experts)
    cols = width // PIECES
    block = (experts, PIECES * cap, cols)
    routing_t, gates_t = routing.T, gates.T
    h = jnp.transpose(hidden[0, 0], (1, 0, 2)).reshape(cap * experts, units)
    vmem = pl.BlockSpec(memory_space=pltpu.VMEM)
    anywhere = pl.BlockSpec(memory_space=pl.ANY)

    blocks, loc = pl.pallas_call(
        functools.partial(before_kernel, experts, cap, group),
        out_shape=(jax.ShapeDtypeStruct(block, BF16), jax.ShapeDtypeStruct((top, tokens), jnp.int32)),
        in_specs=[vmem] * 3,
        out_specs=(vmem, vmem),
        scratch_shapes=[pltpu.VMEM((top * tokens, width), BF16), pltpu.VMEM((experts * cap, width), BF16)],
        name="pack",
    )(routing_t, gates_t, dout)

    half = chips // 2
    plan, _, total = plan_of(half)
    piece = width // groups_dp
    back, grad_hidden, grad_down = pl.pallas_call(
        functools.partial(exchange_kernel, chips, groups_dp, cap, group, lead),
        out_shape=(jax.ShapeDtypeStruct(block, BF16), jax.ShapeDtypeStruct((cap * experts, units), BF16),
                   jax.ShapeDtypeStruct((units, piece), F32)),
        in_specs=[anywhere] * 3,
        out_specs=(vmem, vmem, vmem),
        scratch_shapes=[
            pltpu.VMEM(block, BF16),
            pltpu.VMEM((cap * experts, units), BF16),
            pltpu.VMEM((units, cap * experts), BF16),
            pltpu.VMEM((units, width), BF16),
            pltpu.VMEM(block, BF16),
            pltpu.VMEM(block, BF16),
            pltpu.VMEM((cap * experts, width), BF16),
            pltpu.VMEM((groups_dp, units, piece), BF16),
            pltpu.VMEM((groups_dp - 1, units, piece), BF16),
            pltpu.VMEM((2, 2, 2 * total, PIECES * cap, cols), BF16),
            pltpu.VMEM((2, 2, 2 * (half - 1), PIECES * cap, cols // 2), BF16),
            pltpu.SemaphoreType.DMA((2, 2, half, len(plan))),
            pltpu.SemaphoreType.DMA((2, 2, 3)),
            pltpu.SemaphoreType.DMA((2,)),
            pltpu.SemaphoreType.DMA,
            pltpu.SemaphoreType.DMA,
            pltpu.SemaphoreType.DMA((3,)),
        ],
        compiler_params=pltpu.CompilerParams(collective_id=0, has_side_effects=True, vmem_limit_bytes=62 * 1024 * 1024),
        name="exchange",
    )(blocks, h, w_down[0])

    combined, grad_gates = pl.pallas_call(
        functools.partial(after_kernel, experts, cap, group),
        out_shape=(jax.ShapeDtypeStruct((tokens, width), BF16), jax.ShapeDtypeStruct((top, tokens), F32)),
        in_specs=[vmem] * 4,
        out_specs=(vmem, vmem),
        scratch_shapes=[pltpu.VMEM((experts * cap, width), BF16)],
        name="combine",
    )(back, loc, gates_t, dout)
    grad_hidden = jnp.transpose(grad_hidden.reshape(cap, experts, units), (1, 0, 2))
    return combined, grad_gates.T, grad_hidden[None, None], grad_down[None]


def solution(mesh):
    chips, groups_dp = mesh.shape["expert"] // 2, mesh.shape["dp"]
    half = chips // 2
    lead = max(1, half // 2)
    placed = (
        P(("dp", "expert"), None),
        P(("dp", "expert"), None),
        P("dp", "expert", None, None, None),
        P("expert", None, None),
        P(("dp", "expert"), None),
    )
    return jax.shard_map(
        functools.partial(on_device, chips, groups_dp, lead),
        mesh=mesh,
        in_specs=placed,
        out_specs=(
            P(("dp", "expert"), None),
            P(("dp", "expert"), None),
            P("dp", "expert", None, None, None),
            P("expert", None, "dp"),
        ),
        check_vma=False,
    )
```
